256 devices in a mesh: pts: 64 (over z, x, core), blk: 4 (over y).
Axes of the slice: x: 4, y: 4, z: 8, core: 2. Of those that a mesh axis runs over, the one named last changes fastest.
Arguments:
- points: bfloat16 [2097152, 128], P(('pts', 'blk')), may hold values from -1.5 to 1.5
- targets: float32 [2097152, 64], P(('pts', 'blk')), may hold values from -6 to 6
- coefs: float32 [2097152, 64], P(('pts', 'blk')), may hold values from -0.5 to 0.5
- preds: float32 [2097152, 64], P(('pts', 'blk')), may hold values from -32 to 32
- block_inverse: float32 [2048, 2048], P('blk'), may hold values from -0.2 to 2.2
- block_id: int32 [1], replicated, may hold values from 0 to 1023
Outputs:
- new_coefs: float32 [2097152, 64], P(('pts', 'blk'))
- new_preds: float32 [2097152, 64], P(('pts', 'blk'))
The draws below stay inside these ranges and needn't reach their ends.
All inputs are finite; a program needn't handle non-finite values.
Results may differ from the reference program's by a relative error of at most 0.0042.
Values may be sent and summed in bfloat16 or wider, within the bound.
A program may use at most 128 MiB of HBM per device.

```python
import math
import jax
import jax.numpy as jnp
from jax import lax

F = 128
TGT = 64
B = 2048
R_DEV = 8192
NPTS = 2097152


def draw_block_inverse(key, part):
    first_key = jax.random.fold_in(key, 11)
    second_key = jax.random.fold_in(key, 23)
    normals = jnp.clip(jax.random.normal(first_key, (B, B), jnp.float32), -4.0, 4.0)
    diagonal = jnp.exp(jax.random.uniform(second_key, (B,), jnp.float32, minval=math.log(0.5), maxval=math.log(2.0)))
    coupling = (normals + normals.T) * (0.18 / math.sqrt(B))
    return jnp.diag(diagonal) + coupling


def draw_preds(key, part):
    entry_key = jax.random.fold_in(key, 31)
    row_key = jax.random.fold_in(key, 37)
    column_key = jax.random.fold_in(key, 41)
    column_scale = jnp.exp(jax.random.uniform(column_key, (1, TGT), jnp.float32, minval=math.log(0.5), maxval=math.log(2.0)))
    entries = jnp.clip(jax.random.normal(entry_key, (NPTS, TGT), jnp.float32), -4.0, 4.0)
    row_scale = jnp.exp(jax.random.uniform(row_key, (NPTS, 1), jnp.float32, minval=math.log(0.5), maxval=math.log(4.0)))
    return entries * row_scale * column_scale


def block_levels(stream_key, shape, cuts, low, high):
    gain = 1.0
    for dim, blocks in cuts:
        heights = jax.random.uniform(jax.random.fold_in(jax.random.fold_in(stream_key, 6), dim), (blocks,), jnp.float32, low / len(cuts), high / len(cuts))
        gain = gain * jnp.repeat(jnp.exp(heights), shape[dim] // blocks).reshape((-1,) + (1,) * (len(shape) - 1 - dim))
    return gain


def bell_draw(key, dims, scale, bound, cuts=(), dtype=jnp.bfloat16):
    values = scale * jax.random.normal(key, dims, jnp.float32)
    if cuts:
        values = values * block_levels(key, dims, cuts, -0.22, 0.18)
    return jnp.clip(values, -bound, bound).astype(dtype)


def setup_inputs(seed: int = 0) -> dict:
    streams_of = jax.random.split(jax.random.key(seed), 7)
    points = bell_draw(streams_of[0], (NPTS, F), 0.25, 1.5, ((0, 256),))
    targets = bell_draw(streams_of[1], (NPTS, TGT), 1.0, 6.0, ((0, 256),), jnp.float32)
    coefs = bell_draw(streams_of[2], (NPTS, TGT), 0.08, 0.5, ((0, 256),), jnp.float32)
    preds = draw_preds(jax.random.fold_in(streams_of[6], 71), 0)
    block_inverse = draw_block_inverse(jax.random.fold_in(streams_of[6], 71), 0)
    block_id = jax.random.randint(streams_of[5], (1,), 0, NPTS // B).astype(jnp.int32)
    return {"points": points, "targets": targets, "coefs": coefs, "preds": preds, "block_inverse": block_inverse, "block_id": block_id}


damping = 1.0
inverse_width = 0.25


def kernel_rows(centers, others):
    center_wide = centers.astype(jnp.float32)
    other_wide = others.astype(jnp.float32)
    center_squares = jnp.sum(center_wide * center_wide, axis=1)
    point_squares = jnp.sum(other_wide * other_wide, axis=1)
    inner_products = jnp.dot(centers, others.T, preferred_element_type=jnp.float32)
    distance = center_squares[:, None] + point_squares[None, :] - 2.0 * inner_products
    return jnp.exp(-inverse_width * distance).astype(jnp.bfloat16)


def reference(points, targets, coefs, preds, block_inverse, block_id):
    block_start = (block_id[0] * B).astype(jnp.int32)
    centers = lax.dynamic_slice_in_dim(points, block_start, B, 0)
    block_targets = lax.dynamic_slice_in_dim(targets, block_start, B, 0)
    block_coefs = lax.dynamic_slice_in_dim(coefs, block_start, B, 0)
    shards = NPTS // R_DEV
    point_tiles = points.reshape(shards, R_DEV, F)
    coef_tiles = coefs.astype(jnp.bfloat16).reshape(shards, R_DEV, TGT)

    def accumulate(running, pieces):
        kernel = kernel_rows(centers, pieces[0])
        return running + jnp.dot(kernel, pieces[1], preferred_element_type=jnp.float32), None

    summed, unused = lax.scan(accumulate, jnp.zeros((B, TGT), jnp.float32), (point_tiles, coef_tiles))
    residual = block_targets - damping * block_coefs - summed
    update = jnp.dot(block_inverse, residual, precision=lax.Precision.HIGHEST)
    new_coefs = lax.dynamic_update_slice_in_dim(coefs, block_coefs + update, block_start, 0)
    update_half = update.astype(jnp.bfloat16)

    def advance(pieces):
        kernel = kernel_rows(centers, pieces)
        return jnp.dot(kernel.T, update_half, preferred_element_type=jnp.float32)

    shifts = lax.map(advance, point_tiles)
    new_preds = preds + shifts.reshape(NPTS, TGT)
    return (new_coefs, new_preds)
```

```python
import jax
import jax.numpy as jnp
from jax import lax
from jax.experimental import pallas as pl
from jax.experimental.pallas import tpu as pltpu
from jax.sharding import Mesh
from jax.sharding import PartitionSpec as P

AXES = ("z", "x", "c", "y")
MESH = pl.DeviceIdType.MESH
F, T, B, R = 128, 64, 2048, 8192
SLAB = 512
NS = B // SLAB
CHUNK = 2048
NCH = R // CHUNK
PIECE = 64
HALF = B // 2
SCALE = 0.5 * 1.4426950408889634
NT = (((1,), (1,)), ((), ()))
NN = (((1,), (0,)), ((), ()))
f32, bf16 = jnp.float32, jnp.bfloat16


def dg(a, b, dims):
    return lax.dot_general(a, b, dims, preferred_element_type=f32)


def rem(a, n):
    return lax.rem(a, jnp.int32(n))


def div(a, n):
    return lax.div(a, jnp.int32(n))


def extra_columns(rows, norm_first):
    wide = rows.astype(f32)
    half_norm = -0.5 * jnp.sum(wide * wide, axis=1, keepdims=True)
    high = half_norm.astype(bf16).astype(f32)
    rest = half_norm - high
    middle = rest.astype(bf16).astype(f32)
    low = rest - middle
    lane = lax.broadcasted_iota(jnp.int32, rows.shape, 1)
    at = 0 if norm_first else 3
    ones_at = 3 - at
    out = jnp.where((lane >= ones_at) & (lane < ones_at + 3), 1.0, 0.0)
    out = jnp.where(lane == at, high, out)
    out = jnp.where(lane == at + 1, middle, out)
    out = jnp.where(lane == at + 2, low, out)
    return out.astype(bf16)


def kernel(
    bid, pts_hbm, tg_hbm, cf_hbm, pr_hbm, inv_hbm, nc_hbm, np_hbm,
    km, xa, ca, w16, cf, pr, stage, ihi, ilo, own,
    cand, crecv, hb, rbuf, pbuf, zbuf, fbuf,
    part, rs, ysend, ybuf, zsend, zsum, upd, ubuf, ub,
    lsem, asend, arecv, bsend, brecv, gsend, grecv, usend, urecv,
):
    z, x, c, y = (lax.axis_index(a) for a in AXES)
    plane = x * 4 + y
    q = x * 2 + c
    block = bid[0]
    quarter = rem(block, 4)
    owner = div(block, 4)
    oy = rem(owner, 4)
    oc = rem(div(owner, 4), 2)
    ox = rem(div(owner, 8), 4)
    oz = div(owner, 32)
    oplane = ox * 4 + oy

    def weight(a, b):
        return (a == b).astype(jnp.int32)

    owns = weight(oz, z) * weight(ox, x) * weight(oc, c) * weight(oy, y)

    def pick(index, n, read):
        value = read(0).astype(f32) * weight(index, 0).astype(f32)
        for i in range(1, n):
            value = value + read(i).astype(f32) * weight(index, i).astype(f32)
        return value

    def remote(src, dst, ssem, rsem, dz, dx, dc, dy):
        return pltpu.make_async_remote_copy(
            src_ref=src, dst_ref=dst, send_sem=ssem, recv_sem=rsem,
            device_id=(dz, dx, dc, dy), device_id_type=MESH)

    def plane_peer(d):
        return rem(x + div(d, 4), 4), rem(y + rem(d, 4), 4)

    def xc_peer(d):
        peer = rem(q + d, 8)
        return peer, div(peer, 2), rem(peer, 2)

    def loop(low, high, fn):
        lax.fori_loop(low, high, lambda i, t: (fn(i), t)[1], 0)

    def wait_bytes(view, sem):
        pltpu.make_async_copy(view, view, sem).wait()

    points_in = pltpu.make_async_copy(pts_hbm, xa.at[:, pl.ds(0, F)], lsem.at[0])
    points_in.start()
    targets_in = pltpu.make_async_copy(tg_hbm, pr, lsem.at[1])
    targets_in.start()
    coefs_in = pltpu.make_async_copy(cf_hbm, cf, lsem.at[2])
    coefs_in.start()

    barrier = pltpu.get_barrier_semaphore()

    def greet(dz, dx, dc, dy):
        pl.semaphore_signal(barrier, inc=1, device_id=(dz, dx, dc, dy), device_id_type=MESH)

    def greet_plane(d):
        px, py = plane_peer(d)
        greet(z, px, c, py)

    loop(1, 16, greet_plane)
    loop(1, 8, lambda d: greet(rem(z + d, 8), x, c, y))
    loop(0, 4, lambda d: greet(z, rem(x + d, 4), 1 - c, y))

    points_in.wait()

    def local_half(half):
        def read(k):
            return xa[pl.ds(pl.multiple_of(k * B + half * HALF, HALF), HALF), pl.ds(0, F)]

        return pick(quarter, 4, read)

    cand[...] = local_half(1 - c).astype(bf16)
    pl.semaphore_wait(barrier, 26)

    swap = remote(cand, crecv, asend.at[0], arecv.at[0], z, x, 1 - c, y)
    swap.start()
    swap.wait()
    hb[...] = pick(weight(oc, c), 2, lambda k: local_half(c) if k else crecv[...]).astype(bf16)

    def scatter(d):
        px, py = plane_peer(d)
        row = pl.multiple_of((px * 4 + py) * PIECE, PIECE)
        remote(hb.at[pl.ds(row, PIECE), :], rbuf.at[plane], asend.at[1], arecv.at[1], z, px, c, py).start()

    loop(1, 16, scatter)
    rbuf[plane] = hb[pl.ds(pl.multiple_of(plane * PIECE, PIECE), PIECE), :]

    def widen_points(i):
        rows = pl.ds(pl.multiple_of(i * 512, 512), 512)
        xa[rows, pl.ds(F, F)] = extra_columns(xa[rows, pl.ds(0, F)], False)

    loop(0, R // 512, widen_points)

    wait_bytes(rbuf.at[pl.ds(0, 15)], arecv.at[1])
    pbuf[...] = pick(oplane, 16, lambda k: rbuf[k]).astype(bf16)
    zbuf[z] = pbuf[...]

    def along_z(d):
        remote(pbuf, zbuf.at[z], asend.at[2], arecv.at[2], rem(z + d, 8), x, c, y).start()

    loop(1, 8, along_z)

    coefs_in.wait()
    targets_in.wait()

    def narrow(i):
        cols = pl.ds(pl.multiple_of(i * 1024, 1024), 1024)
        w16[:, cols] = cf[:, cols].astype(bf16)

    loop(0, R // 1024, narrow)
    own[...] = pick(quarter, 4, lambda k: pr[:, pl.ds(k * B, B)] - cf[:, pl.ds(k * B, B)]) * owns.astype(f32)
    preds_in = pltpu.make_async_copy(pr_hbm, pr, lsem.at[1])
    preds_in.start()

    wait_bytes(zbuf.at[pl.ds(0, 7)], arecv.at[2])
    fbuf[...] = pick(oz, 8, lambda k: zbuf[k]).astype(bf16)
    my_rows = pl.ds(pl.multiple_of(c * HALF + plane * PIECE, PIECE), PIECE)
    ca[my_rows, pl.ds(0, F)] = fbuf[...]

    def gather(d):
        px, py = plane_peer(d)
        remote(fbuf, ca.at[my_rows, pl.ds(0, F)], asend.at[3], arecv.at[3], z, px, c, py).start()

    loop(1, 16, gather)

    def split_inverse(i):
        rows = pl.ds(pl.multiple_of(i * 128, 128), 128)
        load = pltpu.make_async_copy(inv_hbm.at[rows, :], stage, lsem.at[3])
        load.start()
        load.wait()
        value = stage[...]
        high = value.astype(bf16)
        ihi[rows, :] = high
        ilo[rows, :] = (value - high.astype(f32)).astype(bf16)

    loop(0, SLAB // 128, split_inverse)

    wait_bytes(rbuf.at[pl.ds(0, 15)], arecv.at[3])
    half_rows = pl.ds(pl.multiple_of(c * HALF, HALF), HALF)
    share = remote(ca.at[half_rows, pl.ds(0, F)], ca.at[half_rows, pl.ds(0, F)],
                   asend.at[4], arecv.at[4], z, x, 1 - c, y)
    share.start()
    share.wait()

    def widen_centers(i):
        rows = pl.ds(pl.multiple_of(i * 512, 512), 512)
        ca[rows, pl.ds(F, F)] = extra_columns(ca[rows, pl.ds(0, F)], True)

    loop(0, B // 512, widen_centers)

    def slab_work(s):
        cols = pl.ds(s * SLAB, SLAB)
        part[s] = own[:, cols]

        def step(j):
            rows = pl.ds(pl.multiple_of(j * CHUNK, CHUNK), CHUNK)
            exponent = dg(xa[rows, :], ca[cols, :], NT)
            tile = jnp.exp2(exponent * SCALE).astype(bf16)
            km[rows, cols] = tile
            part[s] -= dg(w16[:, rows], tile, NN)

        loop(0, NCH, step)

        def send(d):
            peer, px, pc = xc_peer(d)
            rows = pl.ds(pl.multiple_of(peer * 8, 8), 8)
            remote(part.at[s, rows, :], rs.at[s, q], bsend.at[s, 0], brecv.at[s, 0], z, px, pc, y).start()

        loop(1, 8, send)
        rs[s, q] = part[s, pl.ds(pl.multiple_of(q * 8, 8), 8), :]

    def total(ref, s, n):
        value = ref[s, 0]
        for i in range(1, n):
            value = value + ref[s, i]
        return value

    def over_y(s):
        wait_bytes(rs.at[s, pl.ds(0, 7)], brecv.at[s, 0])
        value = total(rs, s, 8)
        ysend[s] = value
        ybuf[s, y] = value

        def send(d):
            remote(ysend.at[s], ybuf.at[s, y], bsend.at[s, 1], brecv.at[s, 1], z, x, c, rem(y + d, 4)).start()

        loop(1, 4, send)

    def over_z(s):
        wait_bytes(ybuf.at[s, pl.ds(0, 3)], brecv.at[s, 1])
        value = total(ybuf, s, 4)
        zsend[s] = value
        zsum[s, z] = value

        def send(d):
            remote(zsend.at[s], zsum.at[s, z], bsend.at[s, 2], brecv.at[s, 2], rem(z + d, 8), x, c, y).start()

        loop(1, 8, send)

    def apply_inverse(s):
        wait_bytes(zsum.at[s, pl.ds(0, 7)], brecv.at[s, 2])
        residual = total(zsum, s, 8)
        high = residual.astype(bf16).astype(f32)
        both = jnp.concatenate([high, residual - high], axis=0).astype(bf16)
        cols = pl.ds(s * SLAB, SLAB)
        by_high = dg(both, ihi[:, cols], NT)
        by_low = dg(both, ilo[:, cols], NT)
        add = by_high[0:8] + by_high[8:16] + by_low[0:8]
        upd[...] = add if s == 0 else upd[...] + add

    for t in range(NS + 3):
        if t < NS:
            slab_work(t)
        if 0 <= t - 1 < NS:
            over_y(t - 1)
        if 0 <= t - 2 < NS:
            over_z(t - 2)
        if 0 <= t - 3 < NS:
            apply_inverse(t - 3)

    upd_rows = pl.ds(pl.multiple_of(q * 8, 8), 8)
    ubuf[upd_rows, :] = upd[...]

    def gather_update(d):
        peer, px, pc = xc_peer(d)
        remote(upd, ubuf.at[upd_rows, :], gsend.at[0], grecv.at[0], z, px, pc, y).start()

    loop(1, 8, gather_update)
    wait_bytes(ubuf.at[pl.ds(0, 56), :], grecv.at[0])
    ub[y] = ubuf[...].astype(bf16)

    def share_update(d):
        remote(ub.at[y], ub.at[y], usend.at[d], urecv.at[4 - d], z, x, c, rem(y + d, 4)).start()

    loop(1, 4, share_update)
    preds_in.wait()

    outs = []
    for i, d in enumerate((0, 1, 3, 2)):
        slab = rem(y + d, 4)
        if d:
            wait_bytes(ub.at[slab], urecv.at[d])
        if i == 3:
            for s in range(NS):
                for k in range(4):
                    cols = pl.ds(k * B + s * SLAB, SLAB)
                    cf[:, cols] += ub[s].astype(f32) * (owns * weight(quarter, k)).astype(f32)
            coefs_out = pltpu.make_async_copy(cf, nc_hbm, lsem.at[2])
            coefs_out.start()

        def advance(j, slab=slab):
            rows = pl.ds(pl.multiple_of(j * CHUNK, CHUNK), CHUNK)
            cols = pl.ds(pl.multiple_of(slab * SLAB, SLAB), SLAB)
            pr[:, rows] += dg(ub[slab], km[rows, cols], NT)

        loop(0, NCH, advance)
    preds_out = pltpu.make_async_copy(pr, np_hbm, lsem.at[1])
    preds_out.start()

    wait_bytes(rbuf.at[pl.ds(0, 15)], asend.at[1])
    wait_bytes(zbuf.at[pl.ds(0, 7)], asend.at[2])
    wait_bytes(rbuf.at[pl.ds(0, 15)], asend.at[3])
    for s in range(NS):
        wait_bytes(rs.at[s, pl.ds(0, 7)], bsend.at[s, 0])
        wait_bytes(ybuf.at[s, pl.ds(0, 3)], bsend.at[s, 1])
        wait_bytes(zsum.at[s, pl.ds(0, 7)], bsend.at[s, 2])
    wait_bytes(ubuf.at[pl.ds(0, 56), :], gsend.at[0])
    for d in range(1, 4):
        wait_bytes(ub.at[0], usend.at[d])
    coefs_out.wait()
    preds_out.wait()


def body(points, targets, coefs, preds, block_inverse, block_id):
    hbm = pl.BlockSpec(memory_space=pl.ANY)
    V, D = pltpu.VMEM, pltpu.SemaphoreType.DMA
    new_coefs, new_preds = pl.pallas_call(
        kernel,
        name="ridge_step",
        in_specs=[pl.BlockSpec(memory_space=pltpu.SMEM)] + [hbm] * 5,
        out_specs=[hbm, hbm],
        out_shape=[jax.ShapeDtypeStruct((T, R), f32)] * 2,
        scratch_shapes=[
            V((R, B), bf16), V((R, 2 * F), bf16), V((B, 2 * F), bf16), V((T, R), bf16), V((T, R), f32), V((T, R), f32),
            V((128, B), f32), V((SLAB, B), bf16), V((SLAB, B), bf16), V((T, B), f32),
            V((HALF, F), bf16), V((HALF, F), bf16), V((HALF, F), bf16), V((16, PIECE, F), bf16),
            V((PIECE, F), bf16), V((8, PIECE, F), bf16), V((PIECE, F), bf16),
            V((NS, T, SLAB), f32), V((NS, 8, 8, SLAB), f32), V((NS, 8, SLAB), f32), V((NS, 4, 8, SLAB), f32),
            V((NS, 8, SLAB), f32), V((NS, 8, 8, SLAB), f32), V((8, SLAB), f32), V((T, SLAB), f32), V((4, T, SLAB), bf16),
            D((4,)), D((5,)), D((5,)), D((NS, 3)), D((NS, 3)), D((1,)), D((1,)), D((4,)), D((4,)),
        ],
        compiler_params=pltpu.CompilerParams(collective_id=0, has_side_effects=True, vmem_limit_bytes=61 << 20),
    )(block_id, points, targets.T, coefs.T, preds.T, block_inverse)
    return new_coefs.T, new_preds.T


def solution(mesh):
    split = Mesh(mesh.devices.reshape(8, 4, 2, mesh.shape["blk"]), AXES)
    rows = P(AXES, None)
    return jax.shard_map(
        body, mesh=split, in_specs=(rows, rows, rows, rows, P("y", None), P()), out_specs=(rows, rows), check_vma=False)
```

```python
import jax
import jax.numpy as jnp
from jax import lax
from jax.experimental import pallas as pl
from jax.experimental.pallas import tpu as pltpu
from jax.sharding import Mesh
from jax.sharding import PartitionSpec as P

AXES = ("z", "x", "c", "y")
MESH = pl.DeviceIdType.MESH
F, T, B, R = 128, 64, 2048, 8192
SLAB = 512
NS = B // SLAB
CHUNK = 4096
NCH = R // CHUNK
PIECE = 16
PLANE = 32
LIMIT = 58 << 20
SCALE = 0.5 * 1.4426950408889634
NT = (((1,), (1,)), ((), ()))
NN = (((1,), (0,)), ((), ()))
f32, bf16 = jnp.float32, jnp.bfloat16


def dg(a, b, dims):
    return lax.dot_general(a, b, dims, preferred_element_type=f32)


def rem(a, n):
    return lax.rem(a, jnp.int32(n))


def div(a, n):
    return lax.div(a, jnp.int32(n))


def extra_columns(rows, norm_first):
    wide = rows.astype(f32)
    half_norm = -0.5 * jnp.sum(wide * wide, axis=1, keepdims=True)
    high = half_norm.astype(bf16).astype(f32)
    rest = half_norm - high
    middle = rest.astype(bf16).astype(f32)
    low = rest - middle
    lane = lax.broadcasted_iota(jnp.int32, rows.shape, 1)
    at = 0 if norm_first else 3
    ones_at = 3 - at
    out = jnp.where((lane >= ones_at) & (lane < ones_at + 3), 1.0, 0.0)
    out = jnp.where(lane == at, high, out)
    out = jnp.where(lane == at + 1, middle, out)
    out = jnp.where(lane == at + 2, low, out)
    return out.astype(bf16)


def kernel(
    bid, pts_hbm, tg_hbm, cf_hbm, pr_hbm, inv_hbm, cf, pr,
    km, xa, ca, w16, stage, ihi, ilo, own,
    cand, rbuf, pbuf, zbuf, fbuf,
    part, rs, ysend, ybuf, zsend, zsum, upd, upd16, ubuf, ub,
    lsem, asend, arecv, bsend, brecv, gsend, grecv, usend, urecv,
):
    z, x, c, y = (lax.axis_index(a) for a in AXES)
    me = (x * 4 + y) * 2 + c
    q = x * 2 + c
    block = bid[0]
    quarter = rem(block, 4)
    owner = div(block, 4)
    oy = rem(owner, 4)
    oc = rem(div(owner, 4), 2)
    ox = rem(div(owner, 8), 4)
    oz = div(owner, 32)
    ome = (ox * 4 + oy) * 2 + oc

    def weight(a, b):
        return (a == b).astype(jnp.int32)

    owns = weight(oz, z) * weight(ome, me)

    def pick(index, n, read):
        value = read(0).astype(f32) * weight(index, 0).astype(f32)
        for i in range(1, n):
            value = value + read(i).astype(f32) * weight(index, i).astype(f32)
        return value

    def remote(src, dst, ssem, rsem, dz, dx, dc, dy):
        return pltpu.make_async_remote_copy(
            src_ref=src, dst_ref=dst, send_sem=ssem, recv_sem=rsem,
            device_id=(dz, dx, dc, dy), device_id_type=MESH)

    def plane_peer(d):
        px, py, pc = rem(x + div(d, 8), 4), rem(y + rem(div(d, 2), 4), 4), rem(c + rem(d, 2), 2)
        return (px * 4 + py) * 2 + pc, px, pc, py

    def xc_peer(d):
        peer = rem(q + d, 8)
        return peer, div(peer, 2), rem(peer, 2)

    def loop(low, high, fn):
        lax.fori_loop(low, high, lambda i, t: (fn(i), t)[1], 0)

    def wait_bytes(view, sem):
        pltpu.make_async_copy(view, view, sem).wait()

    points_in = pltpu.make_async_copy(pts_hbm, xa.at[:, pl.ds(0, F)], lsem.at[0])
    points_in.start()
    targets_in = pltpu.make_async_copy(tg_hbm, pr, lsem.at[1])
    targets_in.start()
    coefs_in = pltpu.make_async_copy(cf_hbm, cf, lsem.at[2])
    coefs_in.start()

    def inverse_in(i):
        return pltpu.make_async_copy(inv_hbm.at[pl.ds(i * 128, 128), :], stage.at[i % 2], lsem.at[3 + i % 2])

    inverse_in(0).start()
    inverse_in(1).start()

    barrier = pltpu.get_barrier_semaphore()

    def greet(dz, dx, dc, dy):
        pl.semaphore_signal(barrier, inc=1, device_id=(dz, dx, dc, dy), device_id_type=MESH)

    def greet_plane(d):
        peer, px, pc, py = plane_peer(d)
        greet(z, px, pc, py)

    loop(1, 8, lambda d: greet(rem(z + d, 8), x, c, y))
    loop(1, PLANE, greet_plane)

    def take(k):
        rows = pl.ds(k * SLAB, SLAB)
        cand[rows, :] = pick(quarter, 4, lambda i: xa[pl.ds(i * B + k * SLAB, SLAB), pl.ds(0, F)]).astype(bf16)

    def scatter(k):
        def send(d):
            peer, px, pc, py = plane_peer(d)
            rows = pl.ds(pl.multiple_of(k * SLAB + peer * PIECE, PIECE), PIECE)
            remote(cand.at[rows, :], rbuf.at[k, me], asend.at[k, 0], arecv.at[k, 0], z, px, pc, py).start()

        loop(1, PLANE, send)
        rbuf[k, me] = cand[pl.ds(pl.multiple_of(k * SLAB + me * PIECE, PIECE), PIECE), :]

    def along_z(k):
        wait_bytes(rbuf.at[k, pl.ds(0, PLANE - 1)], arecv.at[k, 0])
        pbuf[k] = pick(ome, PLANE, lambda i: rbuf[k, i]).astype(bf16)
        zbuf[k, z] = pbuf[k]

        def send(d):
            remote(pbuf.at[k], zbuf.at[k, z], asend.at[k, 1], arecv.at[k, 1], rem(z + d, 8), x, c, y).start()

        loop(1, 8, send)

    def gather(k):
        wait_bytes(zbuf.at[k, pl.ds(0, 7)], arecv.at[k, 1])
        fbuf[k] = pick(oz, 8, lambda i: zbuf[k, i]).astype(bf16)
        rows = pl.ds(pl.multiple_of(k * SLAB + me * PIECE, PIECE), PIECE)
        ca[rows, pl.ds(0, F)] = fbuf[k]

        def send(d):
            peer, px, pc, py = plane_peer(d)
            remote(fbuf.at[k], ca.at[rows, pl.ds(0, F)], asend.at[k, 2], arecv.at[k, 2], z, px, pc, py).start()

        loop(1, PLANE, send)

    def finish_centers(k):
        wait_bytes(rbuf.at[k, pl.ds(0, PLANE - 1)], arecv.at[k, 2])
        rows = pl.ds(k * SLAB, SLAB)
        ca[rows, pl.ds(F, F)] = extra_columns(ca[rows, pl.ds(0, F)], True)

    def widen_points(i):
        rows = pl.ds(pl.multiple_of(i * 512, 512), 512)
        xa[rows, pl.ds(F, F)] = extra_columns(xa[rows, pl.ds(0, F)], False)

    def split_inverse(i):
        inverse_in(i).wait()
        rows = pl.ds(i * 128, 128)
        value = stage[i % 2]
        high = value.astype(bf16)
        ihi[rows, :] = high
        ilo[rows, :] = (value - high.astype(f32)).astype(bf16)
        if i + 2 < SLAB // 128:
            inverse_in(i + 2).start()

    def narrow(i):
        cols = pl.ds(pl.multiple_of(i * 1024, 1024), 1024)
        w16[:, cols] = cf[:, cols].astype(bf16)

    points_in.wait()
    take(0)
    pl.semaphore_wait(barrier, PLANE - 1 + 7)
    scatter(0)
    take(1)
    loop(0, R // 1024, widen_points)
    scatter(1)
    take(2)
    take(3)
    along_z(0)
    scatter(2)
    loop(R // 1024, R // 512, widen_points)
    along_z(1)
    scatter(3)
    coefs_in.wait()
    targets_in.wait()
    loop(0, R // 1024, narrow)
    own[...] = pick(quarter, 4, lambda k: pr[:, pl.ds(k * B, B)] - cf[:, pl.ds(k * B, B)]) * owns.astype(f32)
    preds_in = pltpu.make_async_copy(pr_hbm, pr, lsem.at[1])
    preds_in.start()
    gather(0)
    along_z(2)
    split_inverse(0)
    split_inverse(1)
    gather(1)
    along_z(3)
    split_inverse(2)
    split_inverse(3)
    finish_centers(0)

    def slab_work(s):
        cols = pl.ds(s * SLAB, SLAB)
        part[s] = own[:, cols]

        def step(j):
            rows = pl.ds(pl.multiple_of(j * CHUNK, CHUNK), CHUNK)
            exponent = dg(xa[rows, :], ca[cols, :], NT)
            tile = jnp.exp2(exponent * SCALE).astype(bf16)
            km[rows, cols] = tile
            part[s] -= dg(w16[:, rows], tile, NN)

        loop(0, NCH, step)

        def send(d):
            peer, px, pc = xc_peer(d)
            rows = pl.ds(pl.multiple_of(peer * 8, 8), 8)
            remote(part.at[s, rows, :], rs.at[s, q], bsend.at[s, 0], brecv.at[s, 0], z, px, pc, y).start()

        loop(1, 8, send)
        rs[s, q] = part[s, pl.ds(pl.multiple_of(q * 8, 8), 8), :]

    def total(ref, s, n):
        value = ref[s, 0]
        for i in range(1, n):
            value = value + ref[s, i]
        return value

    def over_y(s):
        wait_bytes(rs.at[s, pl.ds(0, 7)], brecv.at[s, 0])
        value = total(rs, s, 8)
        ysend[s] = value
        ybuf[s, y] = value

        def send(d):
            remote(ysend.at[s], ybuf.at[s, y], bsend.at[s, 1], brecv.at[s, 1], z, x, c, rem(y + d, 4)).start()

        loop(1, 4, send)

    def over_z(s):
        wait_bytes(ybuf.at[s, pl.ds(0, 3)], brecv.at[s, 1])
        value = total(ybuf, s, 4)
        zsend[s] = value
        zsum[s, z] = value

        def send(d):
            remote(zsend.at[s], zsum.at[s, z], bsend.at[s, 2], brecv.at[s, 2], rem(z + d, 8), x, c, y).start()

        loop(1, 8, send)

    def apply_inverse(s):
        wait_bytes(zsum.at[s, pl.ds(0, 7)], brecv.at[s, 2])
        residual = total(zsum, s, 8)
        high = residual.astype(bf16).astype(f32)
        both = jnp.concatenate([high, residual - high], axis=0).astype(bf16)
        cols = pl.ds(s * SLAB, SLAB)
        by_high = dg(both, ihi[:, cols], NT)
        by_low = dg(both, ilo[:, cols], NT)
        add = by_high[0:8] + by_high[8:16] + by_low[0:8]
        upd[...] = add if s == 0 else upd[...] + add

    for t in range(NS + 3):
        if t < NS:
            slab_work(t)
        if t == 0:
            gather(2)
            gather(3)
        if t + 1 < NS:
            finish_centers(t + 1)
        if 0 <= t - 1 < NS:
            over_y(t - 1)
        if 0 <= t - 2 < NS:
            over_z(t - 2)
        if 0 <= t - 3 < NS:
            apply_inverse(t - 3)

    upd16[...] = upd[...].astype(bf16)
    ubuf[q] = upd16[...]

    def gather_update(d):
        peer, px, pc = xc_peer(d)
        remote(upd16, ubuf.at[q], gsend.at[0], grecv.at[0], z, px, pc, y).start()

    loop(1, 8, gather_update)
    wait_bytes(ubuf.at[pl.ds(0, 7)], grecv.at[0])
    ub[y] = jnp.concatenate([ubuf[i].astype(f32) for i in range(8)], axis=0).astype(bf16)

    def share_update(d):
        remote(ub.at[y], ub.at[y], usend.at[0], urecv.at[0], z, x, c, rem(y + d, 4)).start()

    loop(1, 4, share_update)
    preds_in.wait()

    def product(rows, slabs):
        total = None
        for slab in slabs:
            cols = pl.ds(pl.multiple_of(slab * SLAB, SLAB), SLAB)
            one = dg(km[rows, cols], ub[slab], NT)
            total = one if total is None else total + one
        return total.T

    def advance_own(j):
        rows = pl.ds(pl.multiple_of(j * CHUNK, CHUNK), CHUNK)
        pr[:, rows] += product(rows, (y,))

    loop(0, NCH, advance_own)
    wait_bytes(ub.at[pl.ds(0, 3)], urecv.at[0])
    for s in range(NS):
        for k in range(4):
            cols = pl.ds(k * B + s * SLAB, SLAB)
            cf[:, cols] += ub[s].astype(f32) * (owns * weight(quarter, k)).astype(f32)

    def advance(j):
        rows = pl.ds(pl.multiple_of(j * 2048, 2048), 2048)
        pr[:, rows] += product(rows, tuple(rem(y + d, 4) for d in (1, 2, 3)))

    loop(0, R // 2048, advance)

    for k in range(NS):
        wait_bytes(rbuf.at[k, pl.ds(0, PLANE - 1)], asend.at[k, 0])
        wait_bytes(zbuf.at[k, pl.ds(0, 7)], asend.at[k, 1])
        wait_bytes(rbuf.at[k, pl.ds(0, PLANE - 1)], asend.at[k, 2])
    for s in range(NS):
        wait_bytes(rs.at[s, pl.ds(0, 7)], bsend.at[s, 0])
        wait_bytes(ybuf.at[s, pl.ds(0, 3)], bsend.at[s, 1])
        wait_bytes(zsum.at[s, pl.ds(0, 7)], bsend.at[s, 2])
    wait_bytes(ubuf.at[pl.ds(0, 7)], gsend.at[0])
    wait_bytes(ub.at[pl.ds(0, 3)], usend.at[0])


def write_out(cf, pr, nc_hbm, np_hbm, sem):
    copies = [pltpu.make_async_copy(cf, nc_hbm, sem.at[0]), pltpu.make_async_copy(pr, np_hbm, sem.at[1])]
    for copy in copies:
        copy.start()
    for copy in copies:
        copy.wait()


def body(points, targets, coefs, preds, block_inverse, block_id):
    hbm = pl.BlockSpec(memory_space=pl.ANY)
    vmem = pl.BlockSpec(memory_space=pltpu.VMEM)
    V, D = pltpu.VMEM, pltpu.SemaphoreType.DMA
    new_coefs, new_preds = pl.pallas_call(
        kernel,
        name="ridge_step",
        in_specs=[pl.BlockSpec(memory_space=pltpu.SMEM)] + [hbm] * 5,
        out_specs=[vmem, vmem],
        out_shape=[V((T, R), f32)] * 2,
        scratch_shapes=[
            V((R, B), bf16), V((R, 2 * F), bf16), V((B, 2 * F), bf16), V((T, R), bf16),
            V((2, 128, B), f32), V((SLAB, B), bf16), V((SLAB, B), bf16), V((T, B), f32),
            V((B, F), bf16), V((NS, PLANE, PIECE, F), bf16), V((NS, PIECE, F), bf16), V((NS, 8, PIECE, F), bf16), V((NS, PIECE, F), bf16),
            V((NS, T, SLAB), f32), V((NS, 8, 8, SLAB), f32), V((NS, 8, SLAB), f32), V((NS, 4, 8, SLAB), f32),
            V((NS, 8, SLAB), f32), V((NS, 8, 8, SLAB), f32), V((8, SLAB), f32), V((8, SLAB), bf16), V((8, 8, SLAB), bf16), V((4, T, SLAB), bf16),
            D((5,)), D((NS, 3)), D((NS, 3)), D((NS, 3)), D((NS, 3)), D((1,)), D((1,)), D((1,)), D((1,)),
        ],
        compiler_params=pltpu.CompilerParams(collective_id=0, has_side_effects=True, vmem_limit_bytes=LIMIT),
    )(block_id, points, targets.T, coefs.T, preds.T, block_inverse)
    new_coefs, new_preds = pl.pallas_call(
        write_out,
        name="write_out",
        in_specs=[vmem, vmem],
        out_specs=[hbm, hbm],
        out_shape=[jax.ShapeDtypeStruct((T, R), f32)] * 2,
        scratch_shapes=[D((2,))],
        compiler_params=pltpu.CompilerParams(has_side_effects=True, vmem_limit_bytes=1 << 20),
    )(new_coefs, new_preds)
    return new_coefs.T, new_preds.T


def solution(mesh):
    split = Mesh(mesh.devices.reshape(8, 4, 2, mesh.shape["blk"]), AXES)
    rows = P(AXES, None)
    return jax.shard_map(
        body, mesh=split, in_specs=(rows, rows, rows, rows, P("y", None), P()), out_specs=(rows, rows), check_vma=False)
```

```python
import jax
import jax.numpy as jnp
from jax import lax
from jax.experimental import pallas as pl
from jax.experimental.pallas import tpu as pltpu
from jax.sharding import Mesh
from jax.sharding import PartitionSpec as P

AXES = ("z", "x", "c", "y")
MESH = pl.DeviceIdType.MESH
F, T, B, R = 128, 64, 2048, 8192
SLAB = 512
NS = B // SLAB
CHUNK = 4096
PIECE = 16
PLANE = 16
HALF = SLAB // 2
LIMIT = 50 << 20
FIRST = 6144
STEP = 3072
SCALE = 0.5 * 1.4426950408889634
NT = (((1,), (1,)), ((), ()))
NN = (((1,), (0,)), ((), ()))
f32, bf16 = jnp.float32, jnp.bfloat16


def dg(a, b, dims):
    return lax.dot_general(a, b, dims, preferred_element_type=f32)


def rem(a, n):
    return lax.rem(a, jnp.int32(n))


def div(a, n):
    return lax.div(a, jnp.int32(n))


def extra_columns(rows, norm_first):
    wide = rows.astype(f32)
    half_norm = -0.5 * jnp.sum(wide * wide, axis=1, keepdims=True)
    high = half_norm.astype(bf16).astype(f32)
    rest = half_norm - high
    middle = rest.astype(bf16).astype(f32)
    low = rest - middle
    lane = lax.broadcasted_iota(jnp.int32, rows.shape, 1)
    at = 0 if norm_first else 3
    ones_at = 3 - at
    out = jnp.where((lane >= ones_at) & (lane < ones_at + 3), 1.0, 0.0)
    out = jnp.where(lane == at, high, out)
    out = jnp.where(lane == at + 1, middle, out)
    out = jnp.where(lane == at + 2, low, out)
    return out.astype(bf16)


def slab_cols(s):
    return pl.ds(s * SLAB, SLAB) if isinstance(s, int) else pl.ds(pl.multiple_of(s * SLAB, SLAB), SLAB)


def product(km, ub, rows, slabs):
    total = None
    for slab in slabs:
        one = dg(km[rows, slab_cols(slab)], ub[slab], NT)
        total = one if total is None else total + one
    return total.T


def kernel(
    bid, pts_hbm, tg_hbm, cf_hbm, pr_hbm, inv_hbm, cf, pr, kept, u_out,
    km, xa, ca, w16, stage, ihi, ilo, own,
    cand, crecv, hb, rbuf, pbuf, zbuf, fbuf,
    part, rs, ysend, ybuf, zsend, zsum, upd, upd16, ubuf, ub,
    lsem, asend, arecv, bsend, brecv, gsend, grecv, usend, urecv,
):
    z, x, c, y = (lax.axis_index(a) for a in AXES)
    plane = x * 4 + y
    q = x * 2 + c
    block = bid[0]
    quarter = rem(block, 4)
    owner = div(block, 4)
    oy = rem(owner, 4)
    oc = rem(div(owner, 4), 2)
    ox = rem(div(owner, 8), 4)
    oz = div(owner, 32)
    oplane = ox * 4 + oy

    def weight(a, b):
        return (a == b).astype(jnp.int32)

    owns = weight(oz, z) * weight(oplane, plane) * weight(oc, c)

    def pick(index, n, read):
        value = read(0).astype(f32) * weight(index, 0).astype(f32)
        for i in range(1, n):
            value = value + read(i).astype(f32) * weight(index, i).astype(f32)
        return value

    def remote(src, dst, ssem, rsem, dz, dx, dc, dy):
        return pltpu.make_async_remote_copy(
            src_ref=src, dst_ref=dst, send_sem=ssem, recv_sem=rsem,
            device_id=(dz, dx, dc, dy), device_id_type=MESH)

    def plane_peer(d):
        return rem(x + div(d, 8), 4), rem(c + rem(d, 2), 2), rem(y + rem(div(d, 2), 4), 4)

    def z_peer(i):
        half = div(i, 2)
        return rem(z + 4 + half - rem(i, 2) * (half + div(i + 1, 2)), 8)

    def xc_peers():
        for dx, dc in ((2, 0), (2, 1), (1, 0), (3, 0), (1, 1), (3, 1), (0, 1)):
            px, pc = rem(x + dx, 4), rem(c + dc, 2)
            yield px * 2 + pc, px, pc

    def loop(low, high, fn):
        lax.fori_loop(low, high, lambda i, t: (fn(i), t)[1], 0)

    def wait_bytes(view, sem):
        pltpu.make_async_copy(view, view, sem).wait()

    points_in = pltpu.make_async_copy(pts_hbm, xa.at[:, pl.ds(0, F)], lsem.at[0])
    points_in.start()
    targets_in = pltpu.make_async_copy(tg_hbm, pr, lsem.at[1])
    targets_in.start()
    coefs_in = pltpu.make_async_copy(cf_hbm, cf, lsem.at[2])
    coefs_in.start()

    def inverse_in(i):
        return pltpu.make_async_copy(inv_hbm.at[pl.ds(i * 128, 128), :], stage.at[i % 2], lsem.at[3 + i % 2])

    inverse_in(0).start()
    inverse_in(1).start()

    barrier = pltpu.get_barrier_semaphore()

    def greet(dz, dx, dc, dy):
        pl.semaphore_signal(barrier, inc=1, device_id=(dz, dx, dc, dy), device_id_type=MESH)

    def greet_plane(d):
        greet(z, *plane_peer(d))

    loop(1, 8, lambda d: greet(rem(z + d, 8), x, c, y))
    loop(1, 2 * PLANE, greet_plane)

    my_rows = [pl.ds(pl.multiple_of(k * SLAB + c * HALF + plane * PIECE, PIECE), PIECE) for k in range(NS)]

    def take(k):
        rows = pl.ds(k * SLAB, SLAB)
        cand[rows, :] = pick(quarter, 4, lambda i: xa[pl.ds(i * B + k * SLAB, SLAB), pl.ds(0, F)]).astype(bf16)

    def swap(k):
        rows = pl.ds(pl.multiple_of(k * SLAB + (1 - c) * HALF, HALF), HALF)
        remote(cand.at[rows, :], crecv.at[k], asend.at[k, 3], arecv.at[k, 3], z, x, 1 - c, y).start()

    def scatter(k):
        wait_bytes(crecv.at[k], arecv.at[k, 3])
        own_half = cand[pl.ds(pl.multiple_of(k * SLAB + c * HALF, HALF), HALF), :]
        hb[k] = pick(weight(oc, c), 2, lambda i: own_half if i else crecv[k]).astype(bf16)

        def send(d):
            px, py = rem(x + div(d, 4), 4), rem(y + rem(d, 4), 4)
            rows = pl.ds(pl.multiple_of((px * 4 + py) * PIECE, PIECE), PIECE)
            remote(hb.at[k, rows, :], rbuf.at[k, plane], asend.at[k, 0], arecv.at[k, 0], z, px, c, py).start()

        loop(1, PLANE, send)
        rbuf[k, plane] = hb[k, pl.ds(pl.multiple_of(plane * PIECE, PIECE), PIECE), :]

    def along_z(k):
        wait_bytes(rbuf.at[k, pl.ds(0, PLANE - 1)], arecv.at[k, 0])
        pbuf[k] = pick(oplane, PLANE, lambda i: rbuf[k, i]).astype(bf16)
        zbuf[k, z] = pbuf[k]

        def send(d):
            remote(pbuf.at[k], zbuf.at[k, z], asend.at[k, 1], arecv.at[k, 1], z_peer(d), x, c, y).start()

        loop(0, 7, send)

    def gather(k):
        wait_bytes(zbuf.at[k, pl.ds(0, 7)], arecv.at[k, 1])
        fbuf[k] = pick(oz, 8, lambda i: zbuf[k, i]).astype(bf16)
        ca[my_rows[k], pl.ds(0, F)] = fbuf[k]

        def send(d):
            remote(fbuf.at[k], ca.at[my_rows[k], pl.ds(0, F)], asend.at[k, 2], arecv.at[k, 2], z, *plane_peer(d)).start()

        loop(1, 2 * PLANE, send)

    gathered = ca.at[pl.ds(0, (2 * PLANE - 1) * PIECE), pl.ds(0, F)]

    def finish_centers(k):
        wait_bytes(gathered, arecv.at[k, 2])
        rows = slab_cols(k)
        ca[rows, pl.ds(F, F)] = extra_columns(ca[rows, pl.ds(0, F)], True)

    def widen_points(i):
        rows = pl.ds(pl.multiple_of(i * 512, 512), 512)
        xa[rows, pl.ds(F, F)] = extra_columns(xa[rows, pl.ds(0, F)], False)

    def split_inverse(i):
        inverse_in(i).wait()
        rows = pl.ds(i * 128, 128)
        value = stage[i % 2]
        high = value.astype(bf16)
        ihi[rows, :] = high
        ilo[rows, :] = (value - high.astype(f32)).astype(bf16)
        if i + 2 < SLAB // 128:
            inverse_in(i + 2).start()

    def narrow(i):
        cols = pl.ds(pl.multiple_of(i * 1024, 1024), 1024)
        w16[:, cols] = cf[:, cols].astype(bf16)

    points_in.wait()
    for k in range(NS):
        take(k)
    pl.semaphore_wait(barrier, 2 * PLANE - 1 + 7)
    for k in range(NS):
        swap(k)
    scatter(0)
    loop(0, R // 1024, widen_points)
    scatter(1)
    loop(R // 1024, R // 512, widen_points)
    along_z(0)
    scatter(2)
    along_z(1)
    scatter(3)
    coefs_in.wait()
    targets_in.wait()
    loop(0, R // 1024, narrow)
    own[...] = pick(quarter, 4, lambda k: pr[:, pl.ds(k * B, B)] - cf[:, pl.ds(k * B, B)]) * owns.astype(f32)
    preds_in = pltpu.make_async_copy(pr_hbm, pr, lsem.at[1])
    preds_in.start()
    gather(0)
    along_z(2)
    split_inverse(0)
    split_inverse(1)
    gather(1)
    along_z(3)
    split_inverse(2)
    split_inverse(3)
    gather(2)
    finish_centers(0)

    def slab_work(s):
        cols = slab_cols(s)
        part[s] = own[:, cols]

        for low in range(0, R, CHUNK):
            rows = pl.ds(low, CHUNK)
            exponent = dg(xa[rows, :], ca[cols, :], NT)
            tile = jnp.exp2(exponent * SCALE).astype(bf16)
            if low + CHUNK <= FIRST:
                km[rows, cols] = tile
            else:
                km[pl.ds(low, FIRST - low), cols] = tile[: FIRST - low]
                kept[:, cols] = tile[FIRST - low :]
            part[s] -= dg(w16[:, rows], tile, NN)

        for peer, px, pc in xc_peers():
            rows = pl.ds(pl.multiple_of(peer * 8, 8), 8)
            remote(part.at[s, rows, :], rs.at[s, q], bsend.at[s, 0], brecv.at[s, 0], z, px, pc, y).start()
        rs[s, q] = part[s, pl.ds(pl.multiple_of(q * 8, 8), 8), :]

    def total(ref, s, n):
        value = ref[s, 0]
        for i in range(1, n):
            value = value + ref[s, i]
        return value

    def over_y(s):
        wait_bytes(rs.at[s, pl.ds(0, 7)], brecv.at[s, 0])
        value = total(rs, s, 8)
        ysend[s] = value
        ybuf[s, y] = value

        for d in (2, 1, 3):
            remote(ysend.at[s], ybuf.at[s, y], bsend.at[s, 1], brecv.at[s, 1], z, x, c, rem(y + d, 4)).start()

    def over_z(s):
        wait_bytes(ybuf.at[s, pl.ds(0, 3)], brecv.at[s, 1])
        value = total(ybuf, s, 4)
        zsend[s] = value
        zsum[s, z] = value

        def send(d):
            remote(zsend.at[s], zsum.at[s, z], bsend.at[s, 2], brecv.at[s, 2], z_peer(d), x, c, y).start()

        loop(0, 7, send)

    def apply_inverse(s):
        wait_bytes(zsum.at[s, pl.ds(0, 7)], brecv.at[s, 2])
        residual = total(zsum, s, 8)
        high = residual.astype(bf16).astype(f32)
        both = jnp.concatenate([high, residual - high], axis=0).astype(bf16)
        cols = slab_cols(s)
        by_high = dg(both, ihi[:, cols], NT)
        by_low = dg(both, ilo[:, cols], NT)
        upd[...] += by_high[0:8] + by_high[8:16] + by_low[0:8]

    upd[...] = jnp.zeros_like(upd)

    def slab_step(t):
        slab_work(t)
        pl.when(t == 0)(lambda: gather(NS - 1))
        pl.when(t < NS - 1)(lambda: finish_centers(t + 1))
        pl.when(t >= 1)(lambda: over_y(t - 1))
        pl.when(t >= 2)(lambda: over_z(t - 2))

    loop(0, NS, slab_step)
    apply_inverse(0)
    over_y(NS - 1)
    over_z(NS - 2)
    apply_inverse(1)
    over_z(NS - 1)
    apply_inverse(2)
    apply_inverse(3)

    upd16[...] = upd[...].astype(bf16)
    ubuf[q] = upd16[...]

    for peer, px, pc in xc_peers():
        remote(upd16, ubuf.at[q], gsend.at[0], grecv.at[0], z, px, pc, y).start()
    wait_bytes(ubuf.at[pl.ds(0, 7)], grecv.at[0])
    ub[y] = jnp.concatenate([ubuf[i].astype(f32) for i in range(8)], axis=0).astype(bf16)

    def share_update(d):
        kind = d % 2
        remote(ub.at[y], ub.at[y], usend.at[kind], urecv.at[kind], z, x, c, rem(y + d, 4)).start()

    share_update(1)
    share_update(3)
    preds_in.wait()

    def advance(*slabs):
        def step(j):
            rows = pl.ds(pl.multiple_of(j * STEP, STEP), STEP)
            pr[:, rows] += product(km, ub, rows, slabs)

        loop(0, FIRST // STEP, step)

    advance(y)
    share_update(2)
    wait_bytes(ub.at[pl.ds(0, 2)], urecv.at[1])
    advance(rem(y + 1, 4), rem(y + 3, 4))
    wait_bytes(ub.at[0], urecv.at[0])
    for s in range(NS):
        u_out[:, slab_cols(s)] = ub[s]
        for k in range(4):
            cols = pl.ds(k * B + s * SLAB, SLAB)
            cf[:, cols] += ub[s].astype(f32) * (owns * weight(quarter, k)).astype(f32)
    advance(rem(y + 2, 4))

    for k in range(NS):
        wait_bytes(rbuf.at[k, pl.ds(0, PLANE - 1)], asend.at[k, 0])
        wait_bytes(zbuf.at[k, pl.ds(0, 7)], asend.at[k, 1])
        wait_bytes(gathered, asend.at[k, 2])
        wait_bytes(crecv.at[k], asend.at[k, 3])
    for s in range(NS):
        wait_bytes(rs.at[s, pl.ds(0, 7)], bsend.at[s, 0])
        wait_bytes(ybuf.at[s, pl.ds(0, 3)], bsend.at[s, 1])
        wait_bytes(zsum.at[s, pl.ds(0, 7)], bsend.at[s, 2])
    wait_bytes(ubuf.at[pl.ds(0, 7)], gsend.at[0])
    wait_bytes(ub.at[0], usend.at[0])
    wait_bytes(ub.at[pl.ds(0, 2)], usend.at[1])


def finish(cf, pr, kept, u, nc_hbm, np_hbm, out, sem):
    done, rest = pl.ds(0, FIRST), pl.ds(FIRST, R - FIRST)
    copies = [pltpu.make_async_copy(cf, nc_hbm, sem.at[0]), pltpu.make_async_copy(pr.at[:, done], np_hbm.at[:, done], sem.at[1])]
    for copy in copies:
        copy.start()
    out[...] = pr[:, rest] + dg(kept[...], u[...], NT).T
    copies.append(pltpu.make_async_copy(out, np_hbm.at[:, rest], sem.at[2]))
    copies[-1].start()
    for copy in copies:
        copy.wait()


def body(points, targets, coefs, preds, block_inverse, block_id):
    hbm = pl.BlockSpec(memory_space=pl.ANY)
    vmem = pl.BlockSpec(memory_space=pltpu.VMEM)
    V, D = pltpu.VMEM, pltpu.SemaphoreType.DMA
    kept = pl.pallas_call(
        kernel,
        name="ridge_step",
        in_specs=[pl.BlockSpec(memory_space=pltpu.SMEM)] + [hbm] * 5,
        out_specs=[vmem] * 4,
        out_shape=[V((T, R), f32), V((T, R), f32), V((R - FIRST, B), bf16), V((T, B), bf16)],
        scratch_shapes=[
            V((FIRST, B), bf16), V((R, 2 * F), bf16), V((B, 2 * F), bf16), V((T, R), bf16),
            V((2, 128, B), f32), V((SLAB, B), bf16), V((SLAB, B), bf16), V((T, B), f32),
            V((B, F), bf16), V((NS, HALF, F), bf16), V((NS, HALF, F), bf16), V((NS, PLANE, PIECE, F), bf16), V((NS, PIECE, F), bf16), V((NS, 8, PIECE, F), bf16), V((NS, PIECE, F), bf16),
            V((NS, T, SLAB), f32), V((NS, 8, 8, SLAB), f32), V((NS, 8, SLAB), f32), V((NS, 4, 8, SLAB), f32),
            V((NS, 8, SLAB), f32), V((NS, 8, 8, SLAB), f32), V((8, SLAB), f32), V((8, SLAB), bf16), V((8, 8, SLAB), bf16), V((4, T, SLAB), bf16),
            D((5,)), D((NS, 4)), D((NS, 4)), D((NS, 3)), D((NS, 3)), D((1,)), D((1,)), D((2,)), D((2,)),
        ],
        compiler_params=pltpu.CompilerParams(collective_id=0, has_side_effects=True, vmem_limit_bytes=LIMIT),
    )(block_id, points, targets.T, coefs.T, preds.T, block_inverse)
    new_coefs, new_preds = pl.pallas_call(
        finish,
        name="finish",
        in_specs=[vmem] * 4,
        out_specs=[hbm, hbm],
        out_shape=[jax.ShapeDtypeStruct((T, R), f32)] * 2,
        scratch_shapes=[V((T, R - FIRST), f32), D((3,))],
        compiler_params=pltpu.CompilerParams(has_side_effects=True, vmem_limit_bytes=12 << 20),
    )(*kept)
    return new_coefs.T, new_preds.T


def solution(mesh):
    split = Mesh(mesh.devices.reshape(8, 4, 2, mesh.shape["blk"]), AXES)
    rows = P(AXES, None)
    return jax.shard_map(
        body, mesh=split, in_specs=(rows, rows, rows, rows, P("y", None), P()), out_specs=(rows, rows), check_vma=False)
```

```python
import jax
import jax.numpy as jnp
from jax import lax
from jax.experimental import pallas as pl
from jax.experimental.pallas import tpu as pltpu
from jax.sharding import Mesh
from jax.sharding import PartitionSpec as P

AXES = ("z", "x", "c", "y")
MESH = pl.DeviceIdType.MESH
F, T, B, R = 128, 64, 2048, 8192
SLAB = 512
NS = B // SLAB
CHUNK = 4096
PIECE = 16
PLANE = 16
HALF = SLAB // 2
LIMIT = 50 << 20
FIRST = 6144
STEP = 3072
SCALE = 0.5 * 1.4426950408889634
NT = (((1,), (1,)), ((), ()))
NN = (((1,), (0,)), ((), ()))
f32, bf16 = jnp.float32, jnp.bfloat16


def dg(a, b, dims):
    return lax.dot_general(a, b, dims, preferred_element_type=f32)


def rem(a, n):
    return lax.rem(a, jnp.int32(n))


def div(a, n):
    return lax.div(a, jnp.int32(n))


def extra_columns(rows, norm_first):
    wide = rows.astype(f32)
    half_norm = -0.5 * jnp.sum(wide * wide, axis=1, keepdims=True)
    high = half_norm.astype(bf16).astype(f32)
    rest = half_norm - high
    middle = rest.astype(bf16).astype(f32)
    low = rest - middle
    lane = lax.broadcasted_iota(jnp.int32, rows.shape, 1)
    at = 0 if norm_first else 3
    ones_at = 3 - at
    out = jnp.where((lane >= ones_at) & (lane < ones_at + 3), 1.0, 0.0)
    out = jnp.where(lane == at, high, out)
    out = jnp.where(lane == at + 1, middle, out)
    out = jnp.where(lane == at + 2, low, out)
    return out.astype(bf16)


def slab_cols(s):
    return pl.ds(s * SLAB, SLAB) if isinstance(s, int) else pl.ds(pl.multiple_of(s * SLAB, SLAB), SLAB)


def product(km, ub, rows, slabs):
    total = None
    for slab in slabs:
        one = dg(km[rows, slab_cols(slab)], ub[slab], NT)
        total = one if total is None else total + one
    return total.T


def kernel(
    bid, pts_hbm, tg_hbm, cf_hbm, pr_hbm, inv_hbm, cf, pr, kept, u_out,
    km, xa, ca, w16, stage, ihi, ilo, own,
    cand, crecv, hb, rbuf, pbuf, zbuf, fbuf,
    part, rs, ysend, ybuf, zsend, zsum, upd, upd16, ubuf, ub,
    lsem, asend, arecv, bsend, brecv, gsend, grecv, usend, urecv,
):
    z, x, c, y = (lax.axis_index(a) for a in AXES)
    plane = x * 4 + y
    q = x * 2 + c
    block = bid[0]
    quarter = rem(block, 4)
    owner = div(block, 4)
    oy = rem(owner, 4)
    oc = rem(div(owner, 4), 2)
    ox = rem(div(owner, 8), 4)
    oz = div(owner, 32)
    oplane = ox * 4 + oy

    def weight(a, b):
        return (a == b).astype(jnp.int32)

    owns = weight(oz, z) * weight(oplane, plane) * weight(oc, c)

    def pick(index, n, read):
        value = read(0).astype(f32) * weight(index, 0).astype(f32)
        for i in range(1, n):
            value = value + read(i).astype(f32) * weight(index, i).astype(f32)
        return value

    def remote(src, dst, ssem, rsem, dz, dx, dc, dy):
        return pltpu.make_async_remote_copy(
            src_ref=src, dst_ref=dst, send_sem=ssem, recv_sem=rsem,
            device_id=(dz, dx, dc, dy), device_id_type=MESH)

    def to_plane(start):
        for dx in (2, 1, 3, 0):
            px = rem(x + dx, 4)

            def near(i, px=px):
                start(px, rem(c + 1 + rem(i, 2), 2), rem(y + 2 + div(i, 2), 4))

            loop(0, 8 if dx else 5, near)
        start(x, 1 - c, rem(y + 1, 4))
        start(x, c, rem(y + 1, 4))

    def z_peer(i):
        half = div(i, 2)
        return rem(z + 4 + half - rem(i, 2) * (half + div(i + 1, 2)), 8)

    def xc_peers():
        for dx, dc in ((2, 0), (2, 1), (1, 0), (3, 0), (1, 1), (3, 1), (0, 1)):
            px, pc = rem(x + dx, 4), rem(c + dc, 2)
            yield px * 2 + pc, px, pc

    def loop(low, high, fn):
        lax.fori_loop(low, high, lambda i, t: (fn(i), t)[1], 0)

    def wait_bytes(view, sem):
        pltpu.make_async_copy(view, view, sem).wait()

    points_in = pltpu.make_async_copy(pts_hbm, xa.at[:, pl.ds(0, F)], lsem.at[0])
    points_in.start()
    targets_in = pltpu.make_async_copy(tg_hbm, pr, lsem.at[1])
    targets_in.start()
    coefs_in = pltpu.make_async_copy(cf_hbm, cf, lsem.at[2])
    coefs_in.start()

    def inverse_in(i):
        return pltpu.make_async_copy(inv_hbm.at[pl.ds(i * 128, 128), :], stage.at[i % 2], lsem.at[3 + i % 2])

    inverse_in(0).start()
    inverse_in(1).start()

    barrier = pltpu.get_barrier_semaphore()

    def greet(dz, dx, dc, dy):
        pl.semaphore_signal(barrier, inc=1, device_id=(dz, dx, dc, dy), device_id_type=MESH)

    loop(0, 7, lambda i: greet(z_peer(i), x, c, y))
    to_plane(lambda px, pc, py: greet(z, px, pc, py))

    my_rows = [pl.ds(pl.multiple_of(k * SLAB + c * HALF + plane * PIECE, PIECE), PIECE) for k in range(NS)]

    def take(k):
        rows = pl.ds(k * SLAB, SLAB)
        cand[rows, :] = pick(quarter, 4, lambda i: xa[pl.ds(i * B + k * SLAB, SLAB), pl.ds(0, F)]).astype(bf16)

    def swap(k):
        rows = pl.ds(pl.multiple_of(k * SLAB + (1 - c) * HALF, HALF), HALF)
        remote(cand.at[rows, :], crecv.at[k], asend.at[k, 3], arecv.at[k, 3], z, x, 1 - c, y).start()

    def scatter(k):
        wait_bytes(crecv.at[k], arecv.at[k, 3])
        own_half = cand[pl.ds(pl.multiple_of(k * SLAB + c * HALF, HALF), HALF), :]
        hb[k] = pick(weight(oc, c), 2, lambda i: own_half if i else crecv[k]).astype(bf16)

        def send(px, py):
            rows = pl.ds(pl.multiple_of((px * 4 + py) * PIECE, PIECE), PIECE)
            remote(hb.at[k, rows, :], rbuf.at[k, plane], asend.at[k, 0], arecv.at[k, 0], z, px, c, py).start()

        for dx in (2, 1, 3, 0):
            px = rem(x + dx, 4)
            loop(0 if dx else 1, 4, lambda i, px=px, dx=dx: send(px, rem(y + 2 + i, 4) if dx else rem(y + i, 4)))
        rbuf[k, plane] = hb[k, pl.ds(pl.multiple_of(plane * PIECE, PIECE), PIECE), :]

    def along_z(k):
        wait_bytes(rbuf.at[k, pl.ds(0, PLANE - 1)], arecv.at[k, 0])
        pbuf[k] = pick(oplane, PLANE, lambda i: rbuf[k, i]).astype(bf16)
        zbuf[k, z] = pbuf[k]

        def send(d):
            remote(pbuf.at[k], zbuf.at[k, z], asend.at[k, 1], arecv.at[k, 1], z_peer(d), x, c, y).start()

        loop(0, 7, send)

    def gather(k):
        wait_bytes(zbuf.at[k, pl.ds(0, 7)], arecv.at[k, 1])
        fbuf[k] = pick(oz, 8, lambda i: zbuf[k, i]).astype(bf16)
        ca[my_rows[k], pl.ds(0, F)] = fbuf[k]

        to_plane(lambda px, pc, py: remote(
            fbuf.at[k], ca.at[my_rows[k], pl.ds(0, F)], asend.at[k, 2], arecv.at[k, 2], z, px, pc, py).start())

    gathered = ca.at[pl.ds(0, (2 * PLANE - 1) * PIECE), pl.ds(0, F)]

    def finish_centers(k):
        wait_bytes(gathered, arecv.at[k, 2])
        rows = slab_cols(k)
        ca[rows, pl.ds(F, F)] = extra_columns(ca[rows, pl.ds(0, F)], True)

    def widen_points(i):
        rows = pl.ds(pl.multiple_of(i * 512, 512), 512)
        xa[rows, pl.ds(F, F)] = extra_columns(xa[rows, pl.ds(0, F)], False)

    def split_inverse(i):
        inverse_in(i).wait()
        rows = pl.ds(i * 128, 128)
        value = stage[i % 2]
        high = value.astype(bf16)
        ihi[rows, :] = high
        ilo[rows, :] = (value - high.astype(f32)).astype(bf16)
        if i + 2 < SLAB // 128:
            inverse_in(i + 2).start()

    def narrow(i):
        cols = pl.ds(pl.multiple_of(i * 1024, 1024), 1024)
        w16[:, cols] = cf[:, cols].astype(bf16)

    points_in.wait()
    for k in range(NS):
        take(k)
    pl.semaphore_wait(barrier, 2 * PLANE - 1 + 7)
    for k in range(NS):
        swap(k)
    scatter(0)
    loop(0, R // 1024, widen_points)
    scatter(1)
    loop(R // 1024, R // 512, widen_points)
    along_z(0)
    scatter(2)
    along_z(1)
    scatter(3)
    coefs_in.wait()
    targets_in.wait()
    loop(0, R // 1024, narrow)
    own[...] = pick(quarter, 4, lambda k: pr[:, pl.ds(k * B, B)] - cf[:, pl.ds(k * B, B)]) * owns.astype(f32)
    preds_in = pltpu.make_async_copy(pr_hbm, pr, lsem.at[1])
    preds_in.start()
    gather(0)
    along_z(2)
    split_inverse(0)
    split_inverse(1)
    gather(1)
    along_z(3)
    split_inverse(2)
    split_inverse(3)
    gather(2)
    finish_centers(0)

    def slab_work(s):
        cols = slab_cols(s)
        part[s] = own[:, cols]

        for low in range(0, R, CHUNK):
            rows = pl.ds(low, CHUNK)
            exponent = dg(xa[rows, :], ca[cols, :], NT)
            tile = jnp.exp2(exponent * SCALE).astype(bf16)
            if low + CHUNK <= FIRST:
                km[rows, cols] = tile
            else:
                km[pl.ds(low, FIRST - low), cols] = tile[: FIRST - low]
                kept[:, cols] = tile[FIRST - low :]
            part[s] -= dg(w16[:, rows], tile, NN)

        for peer, px, pc in xc_peers():
            rows = pl.ds(pl.multiple_of(peer * 8, 8), 8)
            remote(part.at[s, rows, :], rs.at[s, q], bsend.at[s, 0], brecv.at[s, 0], z, px, pc, y).start()
        rs[s, q] = part[s, pl.ds(pl.multiple_of(q * 8, 8), 8), :]

    def total(ref, s, n):
        value = ref[s, 0]
        for i in range(1, n):
            value = value + ref[s, i]
        return value

    def over_y(s):
        wait_bytes(rs.at[s, pl.ds(0, 7)], brecv.at[s, 0])
        value = total(rs, s, 8)
        ysend[s] = value
        ybuf[s, y] = value

        for d in (2, 1, 3):
            remote(ysend.at[s], ybuf.at[s, y], bsend.at[s, 1], brecv.at[s, 1], z, x, c, rem(y + d, 4)).start()

    def over_z(s):
        wait_bytes(ybuf.at[s, pl.ds(0, 3)], brecv.at[s, 1])
        value = total(ybuf, s, 4)
        zsend[s] = value
        zsum[s, z] = value

        def send(d):
            remote(zsend.at[s], zsum.at[s, z], bsend.at[s, 2], brecv.at[s, 2], z_peer(d), x, c, y).start()

        loop(0, 7, send)

    def apply_inverse(s):
        wait_bytes(zsum.at[s, pl.ds(0, 7)], brecv.at[s, 2])
        residual = total(zsum, s, 8)
        high = residual.astype(bf16).astype(f32)
        both = jnp.concatenate([high, residual - high], axis=0).astype(bf16)
        cols = slab_cols(s)
        by_high = dg(both, ihi[:, cols], NT)
        by_low = dg(both, ilo[:, cols], NT)
        upd[...] += by_high[0:8] + by_high[8:16] + by_low[0:8]

    upd[...] = jnp.zeros_like(upd)

    def slab_step(t):
        slab_work(t)
        pl.when(t == 0)(lambda: gather(NS - 1))
        pl.when(t < NS - 1)(lambda: finish_centers(t + 1))
        pl.when(t >= 1)(lambda: over_y(t - 1))
        pl.when(t >= 2)(lambda: over_z(t - 2))

    loop(0, NS, slab_step)
    apply_inverse(0)
    over_y(NS - 1)
    over_z(NS - 2)
    apply_inverse(1)
    over_z(NS - 1)
    apply_inverse(2)
    apply_inverse(3)

    upd16[...] = upd[...].astype(bf16)
    ubuf[q] = upd16[...]

    for peer, px, pc in xc_peers():
        remote(upd16, ubuf.at[q], gsend.at[0], grecv.at[0], z, px, pc, y).start()
    wait_bytes(ubuf.at[pl.ds(0, 7)], grecv.at[0])
    ub[y] = jnp.concatenate([ubuf[i].astype(f32) for i in range(8)], axis=0).astype(bf16)

    def share_update(d):
        kind = d % 2
        remote(ub.at[y], ub.at[y], usend.at[kind], urecv.at[kind], z, x, c, rem(y + d, 4)).start()

    share_update(1)
    share_update(3)
    preds_in.wait()

    def advance(*slabs):
        def step(j):
            rows = pl.ds(pl.multiple_of(j * STEP, STEP), STEP)
            pr[:, rows] += product(km, ub, rows, slabs)

        loop(0, FIRST // STEP, step)

    advance(y)
    share_update(2)
    rest = pl.ds(FIRST, R - FIRST)
    pr[:, rest] += dg(kept[:, slab_cols(y)], ub[y], NT).T
    wait_bytes(ub.at[pl.ds(0, 2)], urecv.at[1])
    advance(rem(y + 1, 4), rem(y + 3, 4))
    wait_bytes(ub.at[0], urecv.at[0])
    for s in range(NS):
        for k in range(4):
            cols = pl.ds(k * B + s * SLAB, SLAB)
            cf[:, cols] += ub[s].astype(f32) * (owns * weight(quarter, k)).astype(f32)
    u_out[...] = ub[...]
    advance(rem(y + 2, 4))

    for k in range(NS):
        wait_bytes(rbuf.at[k, pl.ds(0, PLANE - 1)], asend.at[k, 0])
        wait_bytes(zbuf.at[k, pl.ds(0, 7)], asend.at[k, 1])
        wait_bytes(gathered, asend.at[k, 2])
        wait_bytes(crecv.at[k], asend.at[k, 3])
    for s in range(NS):
        wait_bytes(rs.at[s, pl.ds(0, 7)], bsend.at[s, 0])
        wait_bytes(ybuf.at[s, pl.ds(0, 3)], bsend.at[s, 1])
        wait_bytes(zsum.at[s, pl.ds(0, 7)], bsend.at[s, 2])
    wait_bytes(ubuf.at[pl.ds(0, 7)], gsend.at[0])
    wait_bytes(ub.at[0], usend.at[0])
    wait_bytes(ub.at[pl.ds(0, 2)], usend.at[1])


def finish(cf, pr, kept, u, nc_hbm, np_hbm, out, sem):
    done, rest = pl.ds(0, FIRST), pl.ds(FIRST, R - FIRST)
    copies = [pltpu.make_async_copy(cf, nc_hbm, sem.at[0]), pltpu.make_async_copy(pr.at[:, done], np_hbm.at[:, done], sem.at[1])]
    for copy in copies:
        copy.start()
    y = lax.axis_index("y")
    out[...] = pr[:, rest] + product(kept, u, pl.ds(0, R - FIRST), tuple(rem(y + d, 4) for d in (1, 2, 3)))
    copies.append(pltpu.make_async_copy(out, np_hbm.at[:, rest], sem.at[2]))
    copies[-1].start()
    for copy in copies:
        copy.wait()


def body(points, targets, coefs, preds, block_inverse, block_id):
    hbm = pl.BlockSpec(memory_space=pl.ANY)
    vmem = pl.BlockSpec(memory_space=pltpu.VMEM)
    V, D = pltpu.VMEM, pltpu.SemaphoreType.DMA
    kept = pl.pallas_call(
        kernel,
        name="ridge_step",
        in_specs=[pl.BlockSpec(memory_space=pltpu.SMEM)] + [hbm] * 5,
        out_specs=[vmem] * 4,
        out_shape=[V((T, R), f32), V((T, R), f32), V((R - FIRST, B), bf16), V((4, T, SLAB), bf16)],
        scratch_shapes=[
            V((FIRST, B), bf16), V((R, 2 * F), bf16), V((B, 2 * F), bf16), V((T, R), bf16),
            V((2, 128, B), f32), V((SLAB, B), bf16), V((SLAB, B), bf16), V((T, B), f32),
            V((B, F), bf16), V((NS, HALF, F), bf16), V((NS, HALF, F), bf16), V((NS, PLANE, PIECE, F), bf16), V((NS, PIECE, F), bf16), V((NS, 8, PIECE, F), bf16), V((NS, PIECE, F), bf16),
            V((NS, T, SLAB), f32), V((NS, 8, 8, SLAB), f32), V((NS, 8, SLAB), f32), V((NS, 4, 8, SLAB), f32),
            V((NS, 8, SLAB), f32), V((NS, 8, 8, SLAB), f32), V((8, SLAB), f32), V((8, SLAB), bf16), V((8, 8, SLAB), bf16), V((4, T, SLAB), bf16),
            D((5,)), D((NS, 4)), D((NS, 4)), D((NS, 3)), D((NS, 3)), D((1,)), D((1,)), D((2,)), D((2,)),
        ],
        compiler_params=pltpu.CompilerParams(collective_id=0, has_side_effects=True, vmem_limit_bytes=LIMIT),
    )(block_id, points, targets.T, coefs.T, preds.T, block_inverse)
    new_coefs, new_preds = pl.pallas_call(
        finish,
        name="finish",
        in_specs=[vmem] * 4,
        out_specs=[hbm, hbm],
        out_shape=[jax.ShapeDtypeStruct((T, R), f32)] * 2,
        scratch_shapes=[V((T, R - FIRST), f32), D((3,))],
        compiler_params=pltpu.CompilerParams(has_side_effects=True, vmem_limit_bytes=12 << 20),
    )(*kept)
    return new_coefs.T, new_preds.T


def solution(mesh):
    split = Mesh(mesh.devices.reshape(8, 4, 2, mesh.shape["blk"]), AXES)
    rows = P(AXES, None)
    return jax.shard_map(
        body, mesh=split, in_specs=(rows, rows, rows, rows, P("y", None), P()), out_specs=(rows, rows), check_vma=False)
```

```python
import jax
import jax.numpy as jnp
from jax import lax
from jax.experimental import pallas as pl
from jax.experimental.pallas import tpu as pltpu
from jax.sharding import Mesh
from jax.sharding import PartitionSpec as P

AXES = ("z", "x", "c", "y")
MESH = pl.DeviceIdType.MESH
F, T, B, R = 128, 64, 2048, 8192
SLAB = 512
NS = B // SLAB
CHUNK = 4096
PIECE = 16
PLANE = 16
HALF = SLAB // 2
LIMIT = 50 << 20
FIRST = 6144
STEP = 3072
SCALE = 0.5 * 1.4426950408889634
NT = (((1,), (1,)), ((), ()))
NN = (((1,), (0,)), ((), ()))
f32, bf16 = jnp.float32, jnp.bfloat16


def dg(a, b, dims):
    return lax.dot_general(a, b, dims, preferred_element_type=f32)


def rem(a, n):
    return lax.rem(a, jnp.int32(n))


def div(a, n):
    return lax.div(a, jnp.int32(n))


def extra_columns(rows, norm_first):
    wide = rows.astype(f32)
    half_norm = -0.5 * jnp.sum(wide * wide, axis=1, keepdims=True)
    high = half_norm.astype(bf16).astype(f32)
    rest = half_norm - high
    middle = rest.astype(bf16).astype(f32)
    low = rest - middle
    lane = lax.broadcasted_iota(jnp.int32, rows.shape, 1)
    at = 0 if norm_first else 3
    ones_at = 3 - at
    out = jnp.where((lane >= ones_at) & (lane < ones_at + 3), 1.0, 0.0)
    out = jnp.where(lane == at, high, out)
    out = jnp.where(lane == at + 1, middle, out)
    out = jnp.where(lane == at + 2, low, out)
    return out.astype(bf16)


def slab_cols(s):
    return pl.ds(s * SLAB, SLAB) if isinstance(s, int) else pl.ds(pl.multiple_of(s * SLAB, SLAB), SLAB)


def product(km, ub, rows, slabs):
    total = None
    for slab in slabs:
        one = dg(km[rows, slab_cols(slab)], ub[slab], NT)
        total = one if total is None else total + one
    return total.T


def kernel(
    bid, pts_hbm, tg_hbm, cf_hbm, pr_hbm, inv_hbm, cf, pr, kept, u_out,
    km, xa, ca, w16, stage, ihi, ilo, own,
    cand, crecv, hb, rbuf, pbuf, zbuf, fbuf,
    part, rs, ysend, ybuf, zsend, zsum, upd, upd16, ubuf, ub,
    lsem, asend, arecv, bsend, brecv, gsend, grecv, usend, urecv,
):
    z, x, c, y = (lax.axis_index(a) for a in AXES)
    plane = x * 4 + y
    q = x * 2 + c
    block = bid[0]
    quarter = rem(block, 4)
    owner = div(block, 4)
    oy = rem(owner, 4)
    oc = rem(div(owner, 4), 2)
    ox = rem(div(owner, 8), 4)
    oz = div(owner, 32)
    oplane = ox * 4 + oy

    def weight(a, b):
        return (a == b).astype(jnp.int32)

    owns = weight(oz, z) * weight(oplane, plane) * weight(oc, c)

    def pick(index, n, read):
        value = read(0).astype(f32) * weight(index, 0).astype(f32)
        for i in range(1, n):
            value = value + read(i).astype(f32) * weight(index, i).astype(f32)
        return value

    def remote(src, dst, ssem, rsem, dz, dx, dc, dy):
        return pltpu.make_async_remote_copy(
            src_ref=src, dst_ref=dst, send_sem=ssem, recv_sem=rsem,
            device_id=(dz, dx, dc, dy), device_id_type=MESH)

    def to_plane(start):
        for dx in (2, 1, 3, 0):
            px = rem(x + dx, 4)

            def near(i, px=px):
                start(px, rem(c + 1 + rem(i, 2), 2), rem(y + 2 + div(i, 2), 4))

            loop(0, 8 if dx else 5, near)
        start(x, 1 - c, rem(y + 1, 4))
        start(x, c, rem(y + 1, 4))

    def z_peer(i):
        half = div(i, 2)
        return rem(z + 4 + half - rem(i, 2) * (half + div(i + 1, 2)), 8)

    def xc_peers():
        for dx, dc in ((2, 0), (2, 1), (1, 0), (3, 0), (1, 1), (3, 1), (0, 1)):
            px, pc = rem(x + dx, 4), rem(c + dc, 2)
            yield px * 2 + pc, px, pc

    def loop(low, high, fn):
        lax.fori_loop(low, high, lambda i, t: (fn(i), t)[1], 0)

    def wait_bytes(view, sem):
        pltpu.make_async_copy(view, view, sem).wait()

    barrier = pltpu.get_barrier_semaphore()

    def greet(dz, dx, dc, dy):
        pl.semaphore_signal(barrier, inc=1, device_id=(dz, dx, dc, dy), device_id_type=MESH)

    loop(0, 7, lambda i: greet(z_peer(i), x, c, y))
    to_plane(lambda px, pc, py: greet(z, px, pc, py))

    points_in = pltpu.make_async_copy(pts_hbm, xa.at[:, pl.ds(0, F)], lsem.at[0])
    points_in.start()
    targets_in = pltpu.make_async_copy(tg_hbm, pr, lsem.at[1])
    targets_in.start()
    coefs_in = pltpu.make_async_copy(cf_hbm, cf, lsem.at[2])
    coefs_in.start()

    def inverse_in(i):
        return pltpu.make_async_copy(inv_hbm.at[pl.ds(i * 128, 128), :], stage.at[i % 2], lsem.at[3 + i % 2])

    inverse_in(0).start()
    inverse_in(1).start()

    my_rows = [pl.ds(pl.multiple_of(k * SLAB + c * HALF + plane * PIECE, PIECE), PIECE) for k in range(NS)]

    def take(k):
        rows = pl.ds(k * SLAB, SLAB)
        cand[rows, :] = pick(quarter, 4, lambda i: xa[pl.ds(i * B + k * SLAB, SLAB), pl.ds(0, F)]).astype(bf16)

    def swap(k):
        rows = pl.ds(pl.multiple_of(k * SLAB + (1 - c) * HALF, HALF), HALF)
        remote(cand.at[rows, :], crecv.at[k], asend.at[k, 3], arecv.at[k, 3], z, x, 1 - c, y).start()

    def scatter(k):
        wait_bytes(crecv.at[k], arecv.at[k, 3])
        own_half = cand[pl.ds(pl.multiple_of(k * SLAB + c * HALF, HALF), HALF), :]
        hb[k] = pick(weight(oc, c), 2, lambda i: own_half if i else crecv[k]).astype(bf16)

        def send(px, py):
            rows = pl.ds(pl.multiple_of((px * 4 + py) * PIECE, PIECE), PIECE)
            remote(hb.at[k, rows, :], rbuf.at[k, plane], asend.at[k, 0], arecv.at[k, 0], z, px, c, py).start()

        for dx in (2, 1, 3, 0):
            px = rem(x + dx, 4)
            loop(0 if dx else 1, 4, lambda i, px=px, dx=dx: send(px, rem(y + 2 + i, 4) if dx else rem(y + i, 4)))
        rbuf[k, plane] = hb[k, pl.ds(pl.multiple_of(plane * PIECE, PIECE), PIECE), :]

    def along_z(k):
        wait_bytes(rbuf.at[k, pl.ds(0, PLANE - 1)], arecv.at[k, 0])
        pbuf[k] = pick(oplane, PLANE, lambda i: rbuf[k, i]).astype(bf16)
        zbuf[k, z] = pbuf[k]

        def send(d):
            remote(pbuf.at[k], zbuf.at[k, z], asend.at[k, 1], arecv.at[k, 1], z_peer(d), x, c, y).start()

        loop(0, 7, send)

    def gather(k):
        wait_bytes(zbuf.at[k, pl.ds(0, 7)], arecv.at[k, 1])
        fbuf[k] = pick(oz, 8, lambda i: zbuf[k, i]).astype(bf16)
        ca[my_rows[k], pl.ds(0, F)] = fbuf[k]

        to_plane(lambda px, pc, py: remote(
            fbuf.at[k], ca.at[my_rows[k], pl.ds(0, F)], asend.at[k, 2], arecv.at[k, 2], z, px, pc, py).start())

    gathered = ca.at[pl.ds(0, (2 * PLANE - 1) * PIECE), pl.ds(0, F)]

    def finish_centers(k):
        wait_bytes(gathered, arecv.at[k, 2])
        rows = slab_cols(k)
        ca[rows, pl.ds(F, F)] = extra_columns(ca[rows, pl.ds(0, F)], True)

    def widen_points(i):
        rows = pl.ds(pl.multiple_of(i * 512, 512), 512)
        xa[rows, pl.ds(F, F)] = extra_columns(xa[rows, pl.ds(0, F)], False)

    def split_inverse(i):
        inverse_in(i).wait()
        rows = pl.ds(i * 128, 128)
        value = stage[i % 2]
        high = value.astype(bf16)
        ihi[rows, :] = high
        ilo[rows, :] = (value - high.astype(f32)).astype(bf16)
        if i + 2 < SLAB // 128:
            inverse_in(i + 2).start()

    def narrow(i):
        cols = pl.ds(pl.multiple_of(i * 1024, 1024), 1024)
        w16[:, cols] = cf[:, cols].astype(bf16)

    points_in.wait()
    for k in range(NS):
        take(k)
    pl.semaphore_wait(barrier, 2 * PLANE - 1 + 7)
    for k in range(NS):
        swap(k)
    scatter(0)
    loop(0, R // 1024, widen_points)
    scatter(1)
    loop(R // 1024, R // 512, widen_points)
    along_z(0)
    scatter(2)
    along_z(1)
    scatter(3)
    coefs_in.wait()
    targets_in.wait()
    loop(0, R // 1024, narrow)
    own[...] = pick(quarter, 4, lambda k: pr[:, pl.ds(k * B, B)] - cf[:, pl.ds(k * B, B)]) * owns.astype(f32)
    preds_in = pltpu.make_async_copy(pr_hbm, pr, lsem.at[1])
    preds_in.start()
    gather(0)
    along_z(2)
    split_inverse(0)
    split_inverse(1)
    gather(1)
    along_z(3)
    split_inverse(2)
    split_inverse(3)
    gather(2)
    finish_centers(0)

    def slab_work(s):
        cols = slab_cols(s)
        part[s] = own[:, cols]

        for low in range(0, R, CHUNK):
            rows = pl.ds(low, CHUNK)
            exponent = dg(xa[rows, :], ca[cols, :], NT)
            tile = jnp.exp2(exponent * SCALE).astype(bf16)
            if low + CHUNK <= FIRST:
                km[rows, cols] = tile
            else:
                km[pl.ds(low, FIRST - low), cols] = tile[: FIRST - low]
                kept[:, cols] = tile[FIRST - low :]
            part[s] -= dg(w16[:, rows], tile, NN)

        for peer, px, pc in xc_peers():
            rows = pl.ds(pl.multiple_of(peer * 8, 8), 8)
            remote(part.at[s, rows, :], rs.at[s, q], bsend.at[s, 0], brecv.at[s, 0], z, px, pc, y).start()
        rs[s, q] = part[s, pl.ds(pl.multiple_of(q * 8, 8), 8), :]

    def total(ref, s, n):
        value = ref[s, 0]
        for i in range(1, n):
            value = value + ref[s, i]
        return value

    def over_y(s):
        wait_bytes(rs.at[s, pl.ds(0, 7)], brecv.at[s, 0])
        value = total(rs, s, 8)
        ysend[s] = value
        ybuf[s, y] = value

        for d in (2, 1, 3):
            remote(ysend.at[s], ybuf.at[s, y], bsend.at[s, 1], brecv.at[s, 1], z, x, c, rem(y + d, 4)).start()

    def over_z(s):
        wait_bytes(ybuf.at[s, pl.ds(0, 3)], brecv.at[s, 1])
        value = total(ybuf, s, 4)
        zsend[s] = value
        zsum[s, z] = value

        def send(d):
            remote(zsend.at[s], zsum.at[s, z], bsend.at[s, 2], brecv.at[s, 2], z_peer(d), x, c, y).start()

        loop(0, 7, send)

    def apply_inverse(s):
        wait_bytes(zsum.at[s, pl.ds(0, 7)], brecv.at[s, 2])
        residual = total(zsum, s, 8)
        high = residual.astype(bf16).astype(f32)
        both = jnp.concatenate([high, residual - high], axis=0).astype(bf16)
        cols = slab_cols(s)
        by_high = dg(both, ihi[:, cols], NT)
        by_low = dg(both, ilo[:, cols], NT)
        upd[...] += by_high[0:8] + by_high[8:16] + by_low[0:8]

    upd[...] = jnp.zeros_like(upd)

    def slab_step(t):
        slab_work(t)
        pl.when(t == 0)(lambda: gather(NS - 1))
        pl.when(t < NS - 1)(lambda: finish_centers(t + 1))
        pl.when(t >= 1)(lambda: over_y(t - 1))
        pl.when(t >= 2)(lambda: over_z(t - 2))

    loop(0, NS, slab_step)
    apply_inverse(0)
    over_y(NS - 1)
    over_z(NS - 2)
    apply_inverse(1)
    over_z(NS - 1)
    apply_inverse(2)
    apply_inverse(3)

    upd16[...] = upd[...].astype(bf16)
    ubuf[q] = upd16[...]

    for peer, px, pc in xc_peers():
        remote(upd16, ubuf.at[q], gsend.at[0], grecv.at[0], z, px, pc, y).start()
    wait_bytes(ubuf.at[pl.ds(0, 7)], grecv.at[0])
    ub[y] = jnp.concatenate([ubuf[i].astype(f32) for i in range(8)], axis=0).astype(bf16)

    def share_update(d):
        kind = d % 2
        remote(ub.at[y], ub.at[y], usend.at[kind], urecv.at[kind], z, x, c, rem(y + d, 4)).start()

    share_update(1)
    share_update(3)
    preds_in.wait()

    def advance(*slabs):
        def step(j):
            rows = pl.ds(pl.multiple_of(j * STEP, STEP), STEP)
            pr[:, rows] += product(km, ub, rows, slabs)

        loop(0, FIRST // STEP, step)

    advance(y)
    share_update(2)
    rest = pl.ds(FIRST, R - FIRST)
    pr[:, rest] += dg(kept[:, slab_cols(y)], ub[y], NT).T
    wait_bytes(ub.at[pl.ds(0, 2)], urecv.at[1])
    advance(rem(y + 1, 4), rem(y + 3, 4))
    wait_bytes(ub.at[0], urecv.at[0])
    for s in range(NS):
        for k in range(4):
            cols = pl.ds(k * B + s * SLAB, SLAB)
            cf[:, cols] += ub[s].astype(f32) * (owns * weight(quarter, k)).astype(f32)
    u_out[...] = ub[...]
    advance(rem(y + 2, 4))

    for k in range(NS):
        wait_bytes(rbuf.at[k, pl.ds(0, PLANE - 1)], asend.at[k, 0])
        wait_bytes(zbuf.at[k, pl.ds(0, 7)], asend.at[k, 1])
        wait_bytes(gathered, asend.at[k, 2])
        wait_bytes(crecv.at[k], asend.at[k, 3])
    for s in range(NS):
        wait_bytes(rs.at[s, pl.ds(0, 7)], bsend.at[s, 0])
        wait_bytes(ybuf.at[s, pl.ds(0, 3)], bsend.at[s, 1])
        wait_bytes(zsum.at[s, pl.ds(0, 7)], bsend.at[s, 2])
    wait_bytes(ubuf.at[pl.ds(0, 7)], gsend.at[0])
    wait_bytes(ub.at[0], usend.at[0])
    wait_bytes(ub.at[pl.ds(0, 2)], usend.at[1])


def finish(cf, pr, kept, u, nc_hbm, np_hbm, out, sem):
    done, rest = pl.ds(0, FIRST), pl.ds(FIRST, R - FIRST)
    copies = [pltpu.make_async_copy(cf, nc_hbm, sem.at[0]), pltpu.make_async_copy(pr.at[:, done], np_hbm.at[:, done], sem.at[1])]
    for copy in copies:
        copy.start()
    y = lax.axis_index("y")
    out[...] = pr[:, rest] + product(kept, u, pl.ds(0, R - FIRST), tuple(rem(y + d, 4) for d in (1, 2, 3)))
    copies.append(pltpu.make_async_copy(out, np_hbm.at[:, rest], sem.at[2]))
    copies[-1].start()
    for copy in copies:
        copy.wait()


def body(points, targets, coefs, preds, block_inverse, block_id):
    hbm = pl.BlockSpec(memory_space=pl.ANY)
    vmem = pl.BlockSpec(memory_space=pltpu.VMEM)
    V, D = pltpu.VMEM, pltpu.SemaphoreType.DMA
    kept = pl.pallas_call(
        kernel,
        name="ridge_step",
        in_specs=[pl.BlockSpec(memory_space=pltpu.SMEM)] + [hbm] * 5,
        out_specs=[vmem] * 4,
        out_shape=[V((T, R), f32), V((T, R), f32), V((R - FIRST, B), bf16), V((4, T, SLAB), bf16)],
        scratch_shapes=[
            V((FIRST, B), bf16), V((R, 2 * F), bf16), V((B, 2 * F), bf16), V((T, R), bf16),
            V((2, 128, B), f32), V((SLAB, B), bf16), V((SLAB, B), bf16), V((T, B), f32),
            V((B, F), bf16), V((NS, HALF, F), bf16), V((NS, HALF, F), bf16), V((NS, PLANE, PIECE, F), bf16), V((NS, PIECE, F), bf16), V((NS, 8, PIECE, F), bf16), V((NS, PIECE, F), bf16),
            V((NS, T, SLAB), f32), V((NS, 8, 8, SLAB), f32), V((NS, 8, SLAB), f32), V((NS, 4, 8, SLAB), f32),
            V((NS, 8, SLAB), f32), V((NS, 8, 8, SLAB), f32), V((8, SLAB), f32), V((8, SLAB), bf16), V((8, 8, SLAB), bf16), V((4, T, SLAB), bf16),
            D((5,)), D((NS, 4)), D((NS, 4)), D((NS, 3)), D((NS, 3)), D((1,)), D((1,)), D((2,)), D((2,)),
        ],
        compiler_params=pltpu.CompilerParams(
            collective_id=0, has_side_effects=True, vmem_limit_bytes=LIMIT),
    )(block_id, points, targets.T, coefs.T, preds.T, block_inverse)
    new_coefs, new_preds = pl.pallas_call(
        finish,
        name="finish",
        in_specs=[vmem] * 4,
        out_specs=[hbm, hbm],
        out_shape=[jax.ShapeDtypeStruct((T, R), f32)] * 2,
        scratch_shapes=[V((T, R - FIRST), f32), D((3,))],
        compiler_params=pltpu.CompilerParams(has_side_effects=True, vmem_limit_bytes=12 << 20),
    )(*kept)
    return new_coefs.T, new_preds.T


def solution(mesh):
    split = Mesh(mesh.devices.reshape(8, 4, 2, mesh.shape["blk"]), AXES)
    rows = P(AXES, None)
    return jax.shard_map(
        body, mesh=split, in_specs=(rows, rows, rows, rows, P("y", None), P()), out_specs=(rows, rows), check_vma=False)
```
